256 devices in a mesh: walker: 64 (over x_hi, y, z), freq: 4 (over x_lo, core).
Axes of the slice: x: 4 (x_hi: 2, x_lo: 2; x = x_hi * 2 + x_lo), y: 4, z: 8, core: 2. Of those that a mesh axis runs over, the one named last changes fastest.
Arguments:
- green_up_blocks: bfloat16 [64, 1, 4, 4288], P('walker', None, 'freq'), may hold values from -6 to 6
- green_down_blocks: bfloat16 [64, 1, 4, 4288], P('walker', None, 'freq'), may hold values from -6 to 6
- nu_index: int32 [4], P('freq'), may hold values from 0 to 3, each once
- q_index: int32 [4], P('freq'), may hold values from 0 to 63
- source: float32 [4, 4096], P('freq', 'walker'), may hold values from -6 to 6
Outputs:
- g4: float32 [4, 4096, 4096], P('freq', 'walker')
- response: float32 [4, 4096], P('freq', 'walker')
The draws below stay inside these ranges and needn't reach their ends.
All inputs are finite; a program needn't handle non-finite values.
Results may differ from the reference program's by a relative error of at most 0.004.
Values may be sent and summed in bfloat16 or wider, within the bound.
No kernel may reach another device: no remote copies, remote signals or barrier semaphores. Data moves between devices by JAX's collectives and lax.ppermute only.
A program may use at most 64 MiB of HBM per device.

```python
import math
import jax
import jax.numpy as jnp
from jax import lax

SIDE = 8
CLUSTER_MOMENTUM = 64
ORBITAL_COUNT = 4
W = 64
NU = 4
WALKER_SAMPLES = 1
ITERS = 2
WALKER_COUNT = 64
BLOCK_FREQUENCY = 67


def set_ends(values, own_key, least, high):
    dims = values.shape
    place = [jax.random.randint(jax.random.fold_in(own_key, axis), (), 0, dims[axis]) for axis in range(len(dims))]
    values = values.at[tuple(place)].set(least)
    longest = dims.index(max(dims))
    place[longest] = (place[longest] + 1) % dims[longest]
    return values.at[tuple(place)].set(high)


def block_scale(stream_key, dims, split, smallest, largest):
    gain = 1.0
    for dim, shards_of in split:
        draws = jax.random.uniform(jax.random.fold_in(jax.random.fold_in(stream_key, 6), dim), (shards_of,), jnp.float32, smallest / len(split), largest / len(split))
        gain = gain * jnp.repeat(jnp.exp(draws), dims[dim] // shards_of).reshape((-1,) + (1,) * (len(dims) - 1 - dim))
    return gain


def centred(rng, dims, spread, limit, shards=(), kind=jnp.bfloat16):
    entries = spread * jax.random.normal(rng, dims, jnp.float32)
    if shards:
        entries = entries * block_scale(rng, dims, shards, -0.22, 0.18)
    return jnp.clip(entries, -limit, limit).astype(kind)


def setup_inputs(seed: int = 0) -> dict:
    splits = jax.random.split(jax.random.key(seed), 6)
    green_up_blocks = centred(splits[0], (WALKER_COUNT, WALKER_SAMPLES, ORBITAL_COUNT, CLUSTER_MOMENTUM * BLOCK_FREQUENCY), 1.0, 6.0, ((0, 64), (2, 4)))
    green_down_blocks = centred(splits[1], (WALKER_COUNT, WALKER_SAMPLES, ORBITAL_COUNT, CLUSTER_MOMENTUM * BLOCK_FREQUENCY), 1.0, 6.0, ((0, 64), (2, 4)))
    nu_index = jax.random.permutation(splits[2], NU).astype(jnp.int32)
    q_index = set_ends(jax.random.randint(splits[3], (NU,), 0, CLUSTER_MOMENTUM), jax.random.fold_in(splits[3], 1), 0, CLUSTER_MOMENTUM - 1).astype(jnp.int32)
    source = centred(splits[4], (NU, CLUSTER_MOMENTUM * W), 1.0, 6.0, ((0, 4), (1, 64)), jnp.float32)
    return {"green_up_blocks": green_up_blocks, "green_down_blocks": green_down_blocks, "nu_index": nu_index, "q_index": q_index, "source": source}


def cluster_sum(sites, shift):
    return (sites // SIDE + shift // SIDE) % SIDE * SIDE + (sites % SIDE + shift % SIDE) % SIDE

def products(block, sites, shift, offset):
    moved = cluster_sum(sites, shift)
    base = jnp.take(block, sites, axis=1)[:, :, :W].astype(jnp.float32)
    other = lax.dynamic_slice_in_dim(jnp.take(block, moved, axis=1), offset, W, 2).astype(jnp.float32)
    return (base * other).astype(jnp.bfloat16).reshape(block.shape[0], sites.shape[0] * W)

def reference(green_up_blocks, green_down_blocks, nu_index, q_index, source):
    sample_count = WALKER_COUNT * WALKER_SAMPLES * ORBITAL_COUNT
    norm = 1.0 / math.sqrt(sample_count)
    scale = 1.0 / (2.0 * math.sqrt(CLUSTER_MOMENTUM * W))
    ups = green_up_blocks.reshape(sample_count, CLUSTER_MOMENTUM, W + NU - 1)
    downs = green_down_blocks.reshape(sample_count, CLUSTER_MOMENTUM, W + NU - 1)
    every = jnp.arange(CLUSTER_MOMENTUM, dtype=jnp.int32)

    def one(packed):
        offset, shift, start = packed
        left = products(ups, every, shift, offset).astype(jnp.float32)
        right = products(downs, every, shift, offset).astype(jnp.float32)
        kernel = jnp.dot(left.T, right, precision=lax.Precision.HIGHEST) * norm
        current = start
        for step in range(ITERS):
            current = start + scale * jnp.dot(current, kernel, precision=lax.Precision.HIGHEST)
        return (kernel, current)
    kernels, answers = lax.map(one, (nu_index, q_index, source))
    return (kernels, answers)
```

```python
import functools
import math

import jax
import jax.numpy as jnp
import numpy as np
from jax import lax
from jax.experimental import pallas as pl
from jax.experimental.pallas import tpu as pltpu
from jax.sharding import Mesh
from jax.sharding import PartitionSpec as P

SIDE = 8
CLUSTER_MOMENTUM = 64
W = 64
NU = 4
ITERS = 2
EXTENT = W + NU - 1
CELLS = CLUSTER_MOMENTUM * W
TAIL = CLUSTER_MOMENTUM * (NU - 1)
GROUP = SIDE * W
UP, DOWN, UP_TAIL, DOWN_TAIL, LOW = 0, CELLS, 2 * CELLS, 2 * CELLS + 256, 2 * CELLS + 512
PACKET = 2 * CELLS + 640
HALF = 128
ROWS = 2 * HALF


def contract(index_ref, own_ref, other_ref, source_ref, g4_ref, out_ref, up, down, left, norm, scale):
    shift_major, shift_minor = index_ref[0] // SIDE, index_ref[0] % SIDE
    offset, site = index_ref[1], index_ref[2]
    halves = (own_ref, other_ref)

    def selector(rows, base, wrapped):
        row = lax.broadcasted_iota(jnp.int32, (rows, GROUP), 0)
        col = lax.broadcasted_iota(jnp.int32, (rows, GROUP), 1)
        minor = (col // W + shift_minor) & (SIDE - 1)
        freq = (col & (W - 1)) + offset
        if wrapped:
            hit = (freq >= W) & (row == base + minor * (NU - 1) + freq - W)
        else:
            hit = (freq < W) & (row == minor * W + freq)
        return hit.astype(jnp.float32).astype(jnp.bfloat16)

    main_select = selector(GROUP, 0, False)

    def build(a, acc):
        moved = (a + shift_major) & (SIDE - 1)
        tail_select = selector(256, moved * SIDE * (NU - 1), True)
        here = pl.ds(pl.multiple_of(a * GROUP, GROUP), GROUP)
        source = source_ref[:, here]
        parts = []
        for half, ref in enumerate(halves):
            rows = pl.ds(half * HALF, HALF)
            for start, tail, held in ((UP, UP_TAIL, up), (DOWN, DOWN_TAIL, down)):
                base = ref[:, pl.ds(pl.multiple_of(start + a * GROUP, GROUP), GROUP)]
                far = ref[:, pl.ds(pl.multiple_of(start + moved * GROUP, GROUP), GROUP)]
                other = jnp.dot(far, main_select, preferred_element_type=jnp.float32)
                other += jnp.dot(
                    ref[:, tail : tail + 256], tail_select, preferred_element_type=jnp.float32
                )
                made = (base.astype(jnp.float32) * other).astype(jnp.bfloat16)
                held[rows, here] = made
                if held is up:
                    weighted = made.astype(jnp.float32) * source
                    parts.append(sum(weighted[:, i : i + 128] for i in range(0, GROUP, 128)))
        return acc + jnp.concatenate(parts, axis=0)

    acc = lax.fori_loop(0, SIDE, build, jnp.zeros((ROWS, 128), jnp.float32))
    first = jnp.sum(acc, axis=1, keepdims=True)

    pair = pl.ds(pl.multiple_of(site // 2 * 128, 128), 128)
    left[...] = up[:, pair].astype(jnp.float32).T
    mine = left[pl.ds(pl.multiple_of(site % 2 * W, W), W), :].astype(jnp.bfloat16)

    def second(a, acc):
        here = pl.ds(pl.multiple_of(a * GROUP, GROUP), GROUP)
        right = down[:, here]
        g4_ref[:, here] = jnp.dot(mine, right, preferred_element_type=jnp.float32) * norm
        moved = jnp.sum(right.astype(jnp.float32) * first, axis=0, keepdims=True)
        current = source_ref[:, here] + (scale * norm) * moved
        weighted = up[:, here].astype(jnp.float32) * current
        return acc + sum(weighted[:, i : i + 128] for i in range(0, GROUP, 128))

    acc = lax.fori_loop(0, SIDE, second, jnp.zeros((ROWS, 128), jnp.float32))
    last = jnp.sum(acc, axis=1, keepdims=True)
    final = source_ref[:, pair] + (scale * norm) * jnp.sum(
        down[:, pair].astype(jnp.float32) * last, axis=0, keepdims=True
    )
    out_ref[...] = jnp.where(site % 2 == 1, final[:, W:], final[:, :W])


def shards(green_up_blocks, green_down_blocks, nu_index, q_index, source):
    samples = ROWS
    norm = 1.0 / math.sqrt(samples)
    scale = 1.0 / (2.0 * math.sqrt(CELLS))

    def split(block):
        sites = block.reshape(CLUSTER_MOMENTUM, EXTENT)
        return sites[:, :W].reshape(CELLS), sites[:, W:].reshape(TAIL)

    up_main, up_tail = split(green_up_blocks)
    down_main, down_tail = split(green_down_blocks)
    start = source.reshape(W)
    high = lax.reduce_precision(start, 8, 7)
    middle = lax.reduce_precision(start - high, 8, 7)
    low = start - high - middle
    packet = jnp.concatenate(
        [
            up_main,
            down_main,
            up_tail,
            high.astype(jnp.bfloat16),
            down_tail,
            middle.astype(jnp.bfloat16),
            low.astype(jnp.bfloat16),
            jnp.zeros((64,), jnp.bfloat16),
        ]
    ).reshape(PACKET // 128, 128)
    along = lax.all_to_all(jnp.broadcast_to(packet, (8,) + packet.shape), "z", 0, 0)
    rows = along.reshape(8, PACKET)
    own = lax.all_to_all(jnp.broadcast_to(rows, (16,) + rows.shape), ("x_hi", "x_lo", "y"), 0, 0)
    own = own.reshape(HALF, PACKET)
    other = lax.ppermute(own, "core", [(0, 1), (1, 0)])
    pieces = own.reshape(2, 2, 32, PACKET)[:, :, :, 2 * CELLS :]
    pieces = lax.dynamic_index_in_dim(pieces, lax.axis_index("x_lo"), 1, False)
    pieces = pieces.reshape(CLUSTER_MOMENTUM, 640).astype(jnp.float32)
    whole = (pieces[:, 192:256] + pieces[:, 448:512]) + pieces[:, 512:576]
    whole = whole.reshape(1, CELLS)
    site = (lax.axis_index("x_hi") * 4 + lax.axis_index("y")) * 8 + lax.axis_index("z")
    index = jnp.stack([q_index[0], nu_index[0], site.astype(jnp.int32)])
    g4, answer = pl.pallas_call(
        functools.partial(contract, norm=norm, scale=scale),
        out_shape=(
            jax.ShapeDtypeStruct((W, CELLS), jnp.float32),
            jax.ShapeDtypeStruct((1, W), jnp.float32),
        ),
        in_specs=[
            pl.BlockSpec(memory_space=pltpu.SMEM),
            pl.BlockSpec(memory_space=pltpu.VMEM),
            pl.BlockSpec(memory_space=pltpu.VMEM),
            pl.BlockSpec(memory_space=pltpu.VMEM),
        ],
        out_specs=(
            pl.BlockSpec(memory_space=pltpu.VMEM),
            pl.BlockSpec(memory_space=pltpu.VMEM),
        ),
        scratch_shapes=[
            pltpu.VMEM((ROWS, CELLS), jnp.bfloat16),
            pltpu.VMEM((ROWS, CELLS), jnp.bfloat16),
            pltpu.VMEM((128, ROWS), jnp.float32),
        ],
        compiler_params=pltpu.CompilerParams(vmem_limit_bytes=48 * 1024 * 1024),
    )(index, own, other, whole)
    return g4.reshape(1, W, CELLS), answer


def solution(mesh):
    fine = Mesh(
        np.asarray(mesh.devices).reshape(2, 4, 8, 2, 2), ("x_hi", "y", "z", "x_lo", "core")
    )
    walker, freq = ("x_hi", "y", "z"), ("x_lo", "core")
    in_specs = (
        P(walker, None, freq, None),
        P(walker, None, freq, None),
        P(freq),
        P(freq),
        P(freq, walker),
    )
    out_specs = (P(freq, walker, None), P(freq, walker))
    return jax.shard_map(shards, mesh=fine, in_specs=in_specs, out_specs=out_specs, check_vma=False)
```

```python
import functools
import math

import jax
import jax.numpy as jnp
import numpy as np
from jax import lax
from jax.experimental import pallas as pl
from jax.experimental.pallas import tpu as pltpu
from jax.sharding import Mesh
from jax.sharding import PartitionSpec as P

SIDE = 8
CLUSTER_MOMENTUM = 64
W = 64
NU = 4
ITERS = 2
EXTENT = W + NU - 1
CELLS = CLUSTER_MOMENTUM * W
TAIL = CLUSTER_MOMENTUM * (NU - 1)
GROUP = SIDE * W
UP, DOWN, UP_TAIL, DOWN_TAIL, LOW = 0, CELLS, 2 * CELLS, 2 * CELLS + 256, 2 * CELLS + 512
PACKET = 2 * CELLS + 640
HALF = 128
ROWS = 2 * HALF


def gather_products(index_ref, ref, source_ref, up, down, start_row):
    shift_major, shift_minor = index_ref[0] // SIDE, index_ref[0] % SIDE
    offset = index_ref[1]
    rows = pl.ds(start_row, HALF)

    def selector(count, base, wrapped):
        row = lax.broadcasted_iota(jnp.int32, (count, GROUP), 0)
        col = lax.broadcasted_iota(jnp.int32, (count, GROUP), 1)
        minor = (col // W + shift_minor) & (SIDE - 1)
        freq = (col & (W - 1)) + offset
        if wrapped:
            hit = (freq >= W) & (row == base + minor * (NU - 1) + freq - W)
        else:
            hit = (freq < W) & (row == minor * W + freq)
        return hit.astype(jnp.float32).astype(jnp.bfloat16)

    main_select = selector(GROUP, 0, False)

    def build(a, acc):
        moved = (a + shift_major) & (SIDE - 1)
        tail_select = selector(256, moved * SIDE * (NU - 1), True)
        here = pl.ds(pl.multiple_of(a * GROUP, GROUP), GROUP)
        for start, tail, held in ((UP, UP_TAIL, up), (DOWN, DOWN_TAIL, down)):
            base = ref[:, pl.ds(pl.multiple_of(start + a * GROUP, GROUP), GROUP)]
            far = ref[:, pl.ds(pl.multiple_of(start + moved * GROUP, GROUP), GROUP)]
            other = jnp.dot(far, main_select, preferred_element_type=jnp.float32)
            other += jnp.dot(
                ref[:, tail : tail + 256], tail_select, preferred_element_type=jnp.float32
            )
            made = (base.astype(jnp.float32) * other).astype(jnp.bfloat16)
            held[rows, here] = made
            if held is up:
                weighted = made.astype(jnp.float32) * source_ref[:, here]
                acc = acc + sum(weighted[:, i : i + 128] for i in range(0, GROUP, 128))
        return acc

    return lax.fori_loop(0, SIDE, build, jnp.zeros((HALF, 128), jnp.float32))


def prepare(index_ref, own_ref, source_ref, up_ref, down_ref, sums_ref):
    sums_ref[...] = gather_products(index_ref, own_ref, source_ref, up_ref, down_ref, 0)


def contract(
    index_ref, up_ref, down_ref, sums_ref, other_ref, source_ref, g4_ref, out_ref,
    up_other, down_other, left, norm, scale,
):
    site = index_ref[2]
    sums = gather_products(index_ref, other_ref, source_ref, up_other, down_other, 0)
    first = (
        jnp.sum(sums_ref[...], axis=1, keepdims=True),
        jnp.sum(sums, axis=1, keepdims=True),
    )
    ups, downs = (up_ref, up_other), (down_ref, down_other)

    pair = pl.ds(pl.multiple_of(site // 2 * 128, 128), 128)
    mine = []
    for half, ref in enumerate(ups):
        left[...] = ref[:, pair].astype(jnp.float32).T
        mine.append(left[pl.ds(pl.multiple_of(site % 2 * W, W), W), :].astype(jnp.bfloat16))

    def second(a, acc):
        here = pl.ds(pl.multiple_of(a * GROUP, GROUP), GROUP)
        right = [ref[:, here] for ref in downs]
        g4_ref[:, here] = (
            jnp.dot(mine[0], right[0], preferred_element_type=jnp.float32)
            + jnp.dot(mine[1], right[1], preferred_element_type=jnp.float32)
        ) * norm
        moved = sum(r.astype(jnp.float32) * f for r, f in zip(right, first))
        moved = jnp.sum(moved, axis=0, keepdims=True)
        current = source_ref[:, here] + (scale * norm) * moved
        made = []
        for ref, old in zip(ups, acc):
            weighted = ref[:, here].astype(jnp.float32) * current
            made.append(old + sum(weighted[:, i : i + 128] for i in range(0, GROUP, 128)))
        return tuple(made)

    zero = jnp.zeros((HALF, 128), jnp.float32)
    acc = lax.fori_loop(0, SIDE, second, (zero, zero))
    final = sum(
        ref[:, pair].astype(jnp.float32) * jnp.sum(part, axis=1, keepdims=True)
        for ref, part in zip(downs, acc)
    )
    final = source_ref[:, pair] + (scale * norm) * jnp.sum(final, axis=0, keepdims=True)
    out_ref[...] = jnp.where(site % 2 == 1, final[:, W:], final[:, :W])


def shards(green_up_blocks, green_down_blocks, nu_index, q_index, source):
    samples = ROWS
    norm = 1.0 / math.sqrt(samples)
    scale = 1.0 / (2.0 * math.sqrt(CELLS))

    both = jnp.concatenate(
        [green_up_blocks.reshape(1, -1), green_down_blocks.reshape(1, -1)], axis=0
    )
    sites = both.reshape(2 * CLUSTER_MOMENTUM, EXTENT)
    main = sites[:, :W].reshape(2 * CELLS)
    tails = sites[:, W:].reshape(2, TAIL)
    up_tail, down_tail = tails[0], tails[1]
    start = source.reshape(W)
    high = lax.reduce_precision(start, 8, 7)
    middle = lax.reduce_precision(start - high, 8, 7)
    low = start - high - middle
    packet = jnp.concatenate(
        [
            main,
            up_tail,
            high.astype(jnp.bfloat16),
            down_tail,
            middle.astype(jnp.bfloat16),
            low.astype(jnp.bfloat16),
            jnp.zeros((64,), jnp.bfloat16),
        ]
    ).reshape(PACKET // 128, 128)
    along = lax.all_to_all(jnp.broadcast_to(packet, (8,) + packet.shape), "z", 0, 0)
    rows = along.reshape(8, PACKET)
    own = lax.all_to_all(jnp.broadcast_to(rows, (16,) + rows.shape), ("x_hi", "x_lo", "y"), 0, 0)
    own = own.reshape(HALF, PACKET)
    other = lax.ppermute(own, "core", [(0, 1), (1, 0)])
    pieces = own.reshape(2, 2, 32, PACKET)[:, :, :, 2 * CELLS :]
    pieces = lax.dynamic_index_in_dim(pieces, lax.axis_index("x_lo"), 1, False)
    pieces = pieces.reshape(CLUSTER_MOMENTUM, 640).astype(jnp.float32)
    whole = (pieces[:, 192:256] + pieces[:, 448:512]) + pieces[:, 512:576]
    whole = whole.reshape(1, CELLS)
    site = (lax.axis_index("x_hi") * 4 + lax.axis_index("y")) * 8 + lax.axis_index("z")
    index = jnp.stack([q_index[0], nu_index[0], site.astype(jnp.int32)])
    vmem = pl.BlockSpec(memory_space=pltpu.VMEM)
    smem = pl.BlockSpec(memory_space=pltpu.SMEM)
    limit = pltpu.CompilerParams(vmem_limit_bytes=48 * 1024 * 1024)
    up, down, sums = pl.pallas_call(
        prepare,
        out_shape=(
            jax.ShapeDtypeStruct((HALF, CELLS), jnp.bfloat16),
            jax.ShapeDtypeStruct((HALF, CELLS), jnp.bfloat16),
            jax.ShapeDtypeStruct((HALF, 128), jnp.float32),
        ),
        in_specs=[smem, vmem, vmem],
        out_specs=(vmem, vmem, vmem),
        compiler_params=limit,
    )(index, own, whole)
    g4, answer = pl.pallas_call(
        functools.partial(contract, norm=norm, scale=scale),
        out_shape=(
            jax.ShapeDtypeStruct((W, CELLS), jnp.float32),
            jax.ShapeDtypeStruct((1, W), jnp.float32),
        ),
        in_specs=[smem, vmem, vmem, vmem, vmem, vmem],
        out_specs=(vmem, vmem),
        scratch_shapes=[
            pltpu.VMEM((HALF, CELLS), jnp.bfloat16),
            pltpu.VMEM((HALF, CELLS), jnp.bfloat16),
            pltpu.VMEM((128, HALF), jnp.float32),
        ],
        compiler_params=limit,
    )(index, up, down, sums, other, whole)
    return g4.reshape(1, W, CELLS), answer


def solution(mesh):
    fine = Mesh(
        np.asarray(mesh.devices).reshape(2, 4, 8, 2, 2), ("x_hi", "y", "z", "x_lo", "core")
    )
    walker, freq = ("x_hi", "y", "z"), ("x_lo", "core")
    in_specs = (
        P(walker, None, freq, None),
        P(walker, None, freq, None),
        P(freq),
        P(freq),
        P(freq, walker),
    )
    out_specs = (P(freq, walker, None), P(freq, walker))
    return jax.shard_map(shards, mesh=fine, in_specs=in_specs, out_specs=out_specs, check_vma=False)
```

```python
import functools
import math

import jax
import jax.numpy as jnp
import numpy as np
from jax import lax
from jax.experimental import pallas as pl
from jax.experimental.pallas import tpu as pltpu
from jax.sharding import Mesh
from jax.sharding import PartitionSpec as P

SIDE = 8
CLUSTER_MOMENTUM = 64
W = 64
NU = 4
ITERS = 2
EXTENT = W + NU - 1
CELLS = CLUSTER_MOMENTUM * W
TAIL = CLUSTER_MOMENTUM * (NU - 1)
GROUP = SIDE * W
UP, DOWN, UP_TAIL, DOWN_TAIL, LOW = 0, CELLS, 2 * CELLS, 2 * CELLS + 256, 2 * CELLS + 512
PACKET = 2 * CELLS + 640
HALF = 128
ROWS = 2 * HALF


def gather_products(index_ref, ref, source_ref, up, down, start_row):
    shift_major, shift_minor = index_ref[0] // SIDE, index_ref[0] % SIDE
    offset = index_ref[1]
    rows = pl.ds(start_row, HALF)

    lanes = shift_minor * W + offset
    tiles, inner = lanes // 128, lanes % 128
    lane = lax.broadcasted_iota(jnp.int32, (HALF, 128), 1)
    near = lane + inner < 128
    kept = (lane & (W - 1)) + offset < W

    col = lax.broadcasted_iota(jnp.int32, (1, GROUP), 1)
    freq = (col & (W - 1)) + offset
    minor = (col // W + shift_minor) & (SIDE - 1)
    wanted = jnp.where(freq >= W, minor * (NU - 1) + freq - W, -256)
    row = lax.broadcasted_iota(jnp.int32, (256, GROUP), 0)

    def build(a, acc):
        moved = (a + shift_major) & (SIDE - 1)
        tail_select = jnp.where(row == wanted + moved * SIDE * (NU - 1), 1.0, 0.0)
        tail_select = tail_select.astype(jnp.bfloat16)
        for start, tail, held in ((UP, UP_TAIL, up), (DOWN, DOWN_TAIL, down)):
            wrapped = jnp.dot(
                ref[:, tail : tail + 256], tail_select, preferred_element_type=jnp.float32
            )
            turned = []
            for t in range(GROUP // 128):
                begin = start + moved * GROUP + ((t + tiles) & (GROUP // 128 - 1)) * 128
                far = ref[:, pl.ds(pl.multiple_of(begin, 128), 128)].astype(jnp.float32)
                turned.append(pltpu.roll(far, (128 - inner) & 127, 1))
            for t in range(GROUP // 128):
                here = pl.ds(pl.multiple_of(a * GROUP + t * 128, 128), 128)
                base = ref[:, pl.ds(pl.multiple_of(start + a * GROUP + t * 128, 128), 128)]
                other = jnp.where(near, turned[t], turned[(t + 1) % len(turned)])
                other = jnp.where(kept, other, wrapped[:, t * 128 : t * 128 + 128])
                made = (base.astype(jnp.float32) * other).astype(jnp.bfloat16)
                held[rows, here] = made
                if held is up:
                    acc = acc + made.astype(jnp.float32) * source_ref[:, here]
        return acc

    return lax.fori_loop(0, SIDE, build, jnp.zeros((HALF, 128), jnp.float32))


def prepare(index_ref, own_ref, source_ref, up_ref, down_ref, sums_ref):
    sums_ref[...] = gather_products(index_ref, own_ref, source_ref, up_ref, down_ref, 0)


def contract(
    index_ref, up_ref, down_ref, sums_ref, other_ref, source_ref, g4_ref, out_ref,
    up_other, down_other, left, norm, scale,
):
    site = index_ref[2]
    sums = gather_products(index_ref, other_ref, source_ref, up_other, down_other, 0)
    first = (
        jnp.sum(sums_ref[...], axis=1, keepdims=True),
        jnp.sum(sums, axis=1, keepdims=True),
    )
    ups, downs = (up_ref, up_other), (down_ref, down_other)

    pair = pl.ds(pl.multiple_of(site // 2 * 128, 128), 128)
    mine = []
    for half, ref in enumerate(ups):
        left[...] = ref[:, pair].astype(jnp.float32).T
        mine.append(left[pl.ds(pl.multiple_of(site % 2 * W, W), W), :].astype(jnp.bfloat16))

    def second(a, acc):
        here = pl.ds(pl.multiple_of(a * GROUP, GROUP), GROUP)
        right = [ref[:, here] for ref in downs]
        g4_ref[:, here] = (
            jnp.dot(mine[0], right[0], preferred_element_type=jnp.float32)
            + jnp.dot(mine[1], right[1], preferred_element_type=jnp.float32)
        ) * norm
        moved = sum(r.astype(jnp.float32) * f for r, f in zip(right, first))
        moved = jnp.sum(moved, axis=0, keepdims=True)
        current = source_ref[:, here] + (scale * norm) * moved
        made = []
        for ref, old in zip(ups, acc):
            weighted = ref[:, here].astype(jnp.float32) * current
            made.append(old + sum(weighted[:, i : i + 128] for i in range(0, GROUP, 128)))
        return tuple(made)

    zero = jnp.zeros((HALF, 128), jnp.float32)
    acc = lax.fori_loop(0, SIDE, second, (zero, zero))
    final = sum(
        ref[:, pair].astype(jnp.float32) * jnp.sum(part, axis=1, keepdims=True)
        for ref, part in zip(downs, acc)
    )
    final = source_ref[:, pair] + (scale * norm) * jnp.sum(final, axis=0, keepdims=True)
    out_ref[...] = jnp.where(site % 2 == 1, final[:, W:], final[:, :W])


def shards(green_up_blocks, green_down_blocks, nu_index, q_index, source):
    samples = ROWS
    norm = 1.0 / math.sqrt(samples)
    scale = 1.0 / (2.0 * math.sqrt(CELLS))

    both = jnp.concatenate(
        [green_up_blocks.reshape(1, -1), green_down_blocks.reshape(1, -1)], axis=0
    )
    sites = both.reshape(2 * CLUSTER_MOMENTUM, EXTENT)
    main = sites[:, :W].reshape(2 * CELLS)
    tails = sites[:, W:].reshape(2, TAIL)
    up_tail, down_tail = tails[0], tails[1]
    start = source.reshape(W)
    high = lax.reduce_precision(start, 8, 7)
    middle = lax.reduce_precision(start - high, 8, 7)
    low = start - high - middle
    packet = jnp.concatenate(
        [
            main,
            up_tail,
            high.astype(jnp.bfloat16),
            down_tail,
            middle.astype(jnp.bfloat16),
            low.astype(jnp.bfloat16),
            jnp.zeros((64,), jnp.bfloat16),
        ]
    ).reshape(PACKET // 128, 128)
    along = lax.all_to_all(jnp.broadcast_to(packet, (8,) + packet.shape), "z", 0, 0)
    rows = along.reshape(8, PACKET)
    own = lax.all_to_all(jnp.broadcast_to(rows, (16,) + rows.shape), ("x_hi", "x_lo", "y"), 0, 0)
    own = own.reshape(HALF, PACKET)
    other = lax.ppermute(own, "core", [(0, 1), (1, 0)])
    pieces = own.reshape(2, 2, 32, PACKET)[:, :, :, 2 * CELLS :]
    pieces = lax.dynamic_index_in_dim(pieces, lax.axis_index("x_lo"), 1, False)
    pieces = pieces.reshape(CLUSTER_MOMENTUM, 640).astype(jnp.float32)
    whole = (pieces[:, 192:256] + pieces[:, 448:512]) + pieces[:, 512:576]
    whole = whole.reshape(1, CELLS)
    site = (lax.axis_index("x_hi") * 4 + lax.axis_index("y")) * 8 + lax.axis_index("z")
    index = jnp.stack([q_index[0], nu_index[0], site.astype(jnp.int32)])
    vmem = pl.BlockSpec(memory_space=pltpu.VMEM)
    smem = pl.BlockSpec(memory_space=pltpu.SMEM)
    limit = pltpu.CompilerParams(vmem_limit_bytes=48 * 1024 * 1024)
    up, down, sums = pl.pallas_call(
        prepare,
        out_shape=(
            jax.ShapeDtypeStruct((HALF, CELLS), jnp.bfloat16),
            jax.ShapeDtypeStruct((HALF, CELLS), jnp.bfloat16),
            jax.ShapeDtypeStruct((HALF, 128), jnp.float32),
        ),
        in_specs=[smem, vmem, vmem],
        out_specs=(vmem, vmem, vmem),
        compiler_params=limit,
    )(index, own, whole)
    g4, answer = pl.pallas_call(
        functools.partial(contract, norm=norm, scale=scale),
        out_shape=(
            jax.ShapeDtypeStruct((W, CELLS), jnp.float32),
            jax.ShapeDtypeStruct((1, W), jnp.float32),
        ),
        in_specs=[smem, vmem, vmem, vmem, vmem, vmem],
        out_specs=(vmem, vmem),
        scratch_shapes=[
            pltpu.VMEM((HALF, CELLS), jnp.bfloat16),
            pltpu.VMEM((HALF, CELLS), jnp.bfloat16),
            pltpu.VMEM((128, HALF), jnp.float32),
        ],
        compiler_params=limit,
    )(index, up, down, sums, other, whole)
    return g4.reshape(1, W, CELLS), answer


def solution(mesh):
    fine = Mesh(
        np.asarray(mesh.devices).reshape(2, 4, 8, 2, 2), ("x_hi", "y", "z", "x_lo", "core")
    )
    walker, freq = ("x_hi", "y", "z"), ("x_lo", "core")
    in_specs = (
        P(walker, None, freq, None),
        P(walker, None, freq, None),
        P(freq),
        P(freq),
        P(freq, walker),
    )
    out_specs = (P(freq, walker, None), P(freq, walker))
    return jax.shard_map(shards, mesh=fine, in_specs=in_specs, out_specs=out_specs, check_vma=False)
```

```python
import functools
import math

import jax
import jax.numpy as jnp
import numpy as np
from jax import lax
from jax.experimental import pallas as pl
from jax.experimental.pallas import tpu as pltpu
from jax.sharding import Mesh
from jax.sharding import PartitionSpec as P

SIDE = 8
CLUSTER_MOMENTUM = 64
W = 64
NU = 4
ITERS = 2
EXTENT = W + NU - 1
CELLS = CLUSTER_MOMENTUM * W
TAIL = CLUSTER_MOMENTUM * (NU - 1)
GROUP = SIDE * W
UP, DOWN, UP_TAIL, DOWN_TAIL, LOW = 0, CELLS, 2 * CELLS, 2 * CELLS + 256, 2 * CELLS + 512
PACKET = 2 * CELLS + 640
HALF = 128
ROWS = 2 * HALF


def gather_products(index_ref, ref, source_ref, up, down, start_row):
    shift_major, shift_minor = index_ref[0] // SIDE, index_ref[0] % SIDE
    offset = index_ref[1]
    rows = pl.ds(start_row, HALF)

    lanes = shift_minor * W + offset
    tiles, inner = lanes // 128, lanes % 128
    lane = lax.broadcasted_iota(jnp.int32, (HALF, 128), 1)
    near = lane + inner < 128
    kept = (lane & (W - 1)) + offset < W

    col = lax.broadcasted_iota(jnp.int32, (1, GROUP), 1)
    freq = (col & (W - 1)) + offset
    minor = (col // W + shift_minor) & (SIDE - 1)
    wanted = jnp.where(freq >= W, minor * (NU - 1) + freq - W, -256)
    row = lax.broadcasted_iota(jnp.int32, (256, GROUP), 0)

    def build(a, acc):
        moved = (a + shift_major) & (SIDE - 1)
        tail_select = jnp.where(row == wanted + moved * SIDE * (NU - 1), 1.0, 0.0)
        tail_select = tail_select.astype(jnp.bfloat16)
        for start, tail, held in ((UP, UP_TAIL, up), (DOWN, DOWN_TAIL, down)):
            wrapped = jnp.dot(
                ref[:, tail : tail + 256], tail_select, preferred_element_type=jnp.float32
            )
            turned = []
            for t in range(GROUP // 128):
                begin = start + moved * GROUP + ((t + tiles) & (GROUP // 128 - 1)) * 128
                far = ref[:, pl.ds(pl.multiple_of(begin, 128), 128)].astype(jnp.float32)
                turned.append(pltpu.roll(far, (128 - inner) & 127, 1))
            for t in range(GROUP // 128):
                here = pl.ds(pl.multiple_of(a * GROUP + t * 128, 128), 128)
                base = ref[:, pl.ds(pl.multiple_of(start + a * GROUP + t * 128, 128), 128)]
                other = jnp.where(near, turned[t], turned[(t + 1) % len(turned)])
                other = jnp.where(kept, other, wrapped[:, t * 128 : t * 128 + 128])
                made = (base.astype(jnp.float32) * other).astype(jnp.bfloat16)
                held[rows, here] = made
                if held is up:
                    acc = acc + made.astype(jnp.float32) * source_ref[:, here]
        return acc

    return lax.fori_loop(0, SIDE, build, jnp.zeros((HALF, 128), jnp.float32))


def prepare(index_ref, own_ref, source_ref, up_ref, down_ref, sums_ref):
    sums_ref[...] = gather_products(index_ref, own_ref, source_ref, up_ref, down_ref, 0)


def three_rows(row):
    high = row.astype(jnp.bfloat16).astype(jnp.float32)
    middle = (row - high).astype(jnp.bfloat16).astype(jnp.float32)
    low = row - high - middle
    at = lax.broadcasted_iota(jnp.int32, (16, row.shape[1]), 0)
    return jnp.where(
        at == 0, high, jnp.where(at == 1, middle, jnp.where(at == 2, low, 0.0))
    )


def contract(
    index_ref, up_ref, down_ref, sums_ref, other_ref, source_ref, g4_ref, out_ref,
    up_other, down_other, left, stage, sems, norm, scale,
):
    site = index_ref[2]
    sums = gather_products(index_ref, other_ref, source_ref, up_other, down_other, 0)
    first = jnp.concatenate(
        [jnp.sum(part.T, axis=0, keepdims=True) for part in (sums_ref[...], sums)], axis=1
    )
    ups, downs = (up_ref, up_other), (down_ref, down_other)

    pair = pl.ds(pl.multiple_of(site // 2 * 128, 128), 128)
    mine = []
    for ref in ups:
        left[...] = ref[:, pair].astype(jnp.float32).T
        mine.append(left[pl.ds(pl.multiple_of(site % 2 * W, W), W), :])
    lhs = jnp.concatenate([jnp.concatenate(mine, axis=1), three_rows(first)], axis=0)
    lhs = lhs.astype(jnp.bfloat16)

    copies = []
    last = [jnp.zeros((16, HALF), jnp.float32), jnp.zeros((16, HALF), jnp.float32)]
    for a in range(SIDE):
        here = pl.ds(a * GROUP, GROUP)
        right = jnp.concatenate([ref[:, here] for ref in downs], axis=0)
        both = jnp.dot(lhs, right, preferred_element_type=jnp.float32)
        stage[:, here] = both[:W] * norm
        copies.append(
            pltpu.make_async_copy(stage.at[:, here], g4_ref.at[:, here], sems.at[a])
        )
        copies[-1].start()
        moved = jnp.sum(both[W:], axis=0, keepdims=True)
        current = source_ref[:, here] + (scale * norm) * moved
        rows = three_rows(current).astype(jnp.bfloat16)
        for half, ref in enumerate(ups):
            last[half] += lax.dot_general(
                rows, ref[:, here], (((1,), (1,)), ((), ())),
                preferred_element_type=jnp.float32,
            )
    final = jnp.zeros((16, 128), jnp.float32)
    for part, ref in zip(last, downs):
        rows = three_rows(jnp.sum(part, axis=0, keepdims=True)).astype(jnp.bfloat16)
        final += jnp.dot(rows, ref[:, pair], preferred_element_type=jnp.float32)
    final = source_ref[:, pair] + (scale * norm) * jnp.sum(final, axis=0, keepdims=True)
    out_ref[...] = jnp.where(site % 2 == 1, final[:, W:], final[:, :W])
    for copy in copies:
        copy.wait()


def shards(green_up_blocks, green_down_blocks, nu_index, q_index, source):
    samples = ROWS
    norm = 1.0 / math.sqrt(samples)
    scale = 1.0 / (2.0 * math.sqrt(CELLS))

    both = jnp.concatenate(
        [green_up_blocks.reshape(1, -1), green_down_blocks.reshape(1, -1)], axis=0
    )
    sites = both.reshape(2 * CLUSTER_MOMENTUM, EXTENT)
    main = sites[:, :W].reshape(2 * CELLS)
    tails = sites[:, W:].reshape(2, TAIL)
    up_tail, down_tail = tails[0], tails[1]
    start = source.reshape(W)
    high = lax.reduce_precision(start, 8, 7)
    middle = lax.reduce_precision(start - high, 8, 7)
    low = start - high - middle
    packet = jnp.concatenate(
        [
            main,
            up_tail,
            high.astype(jnp.bfloat16),
            down_tail,
            middle.astype(jnp.bfloat16),
            low.astype(jnp.bfloat16),
            jnp.zeros((64,), jnp.bfloat16),
        ]
    ).reshape(PACKET // 128, 128)
    along = lax.all_to_all(jnp.broadcast_to(packet, (8,) + packet.shape), "z", 0, 0)
    rows = along.reshape(8, PACKET)
    own = lax.all_to_all(jnp.broadcast_to(rows, (16,) + rows.shape), ("x_hi", "x_lo", "y"), 0, 0)
    own = own.reshape(HALF, PACKET)
    other = lax.ppermute(own, "core", [(0, 1), (1, 0)])
    pieces = own.reshape(2, 2, 32, PACKET)[:, :, :, 2 * CELLS :]
    pieces = lax.dynamic_index_in_dim(pieces, lax.axis_index("x_lo"), 1, False)
    pieces = pieces.reshape(CLUSTER_MOMENTUM, 640).astype(jnp.float32)
    whole = (pieces[:, 192:256] + pieces[:, 448:512]) + pieces[:, 512:576]
    whole = whole.reshape(1, CELLS)
    site = (lax.axis_index("x_hi") * 4 + lax.axis_index("y")) * 8 + lax.axis_index("z")
    index = jnp.stack([q_index[0], nu_index[0], site.astype(jnp.int32)])
    vmem = pl.BlockSpec(memory_space=pltpu.VMEM)
    smem = pl.BlockSpec(memory_space=pltpu.SMEM)
    limit = pltpu.CompilerParams(vmem_limit_bytes=48 * 1024 * 1024)
    up, down, sums = pl.pallas_call(
        prepare,
        out_shape=(
            jax.ShapeDtypeStruct((HALF, CELLS), jnp.bfloat16),
            jax.ShapeDtypeStruct((HALF, CELLS), jnp.bfloat16),
            jax.ShapeDtypeStruct((HALF, 128), jnp.float32),
        ),
        in_specs=[smem, vmem, vmem],
        out_specs=(vmem, vmem, vmem),
        compiler_params=limit,
    )(index, own, whole)
    g4, answer = pl.pallas_call(
        functools.partial(contract, norm=norm, scale=scale),
        out_shape=(
            jax.ShapeDtypeStruct((W, CELLS), jnp.float32),
            jax.ShapeDtypeStruct((1, W), jnp.float32),
        ),
        in_specs=[smem, vmem, vmem, vmem, vmem, vmem],
        out_specs=(pl.BlockSpec(memory_space=pl.ANY), vmem),
        scratch_shapes=[
            pltpu.VMEM((HALF, CELLS), jnp.bfloat16),
            pltpu.VMEM((HALF, CELLS), jnp.bfloat16),
            pltpu.VMEM((128, HALF), jnp.float32),
            pltpu.VMEM((W, CELLS), jnp.float32),
            pltpu.SemaphoreType.DMA((SIDE,)),
        ],
        compiler_params=limit,
    )(index, up, down, sums, other, whole)
    return g4.reshape(1, W, CELLS), answer


def solution(mesh):
    fine = Mesh(
        np.asarray(mesh.devices).reshape(2, 4, 8, 2, 2), ("x_hi", "y", "z", "x_lo", "core")
    )
    walker, freq = ("x_hi", "y", "z"), ("x_lo", "core")
    in_specs = (
        P(walker, None, freq, None),
        P(walker, None, freq, None),
        P(freq),
        P(freq),
        P(freq, walker),
    )
    out_specs = (P(freq, walker, None), P(freq, walker))
    return jax.shard_map(shards, mesh=fine, in_specs=in_specs, out_specs=out_specs, check_vma=False)
```

```python
import functools
import math

import jax
import jax.numpy as jnp
import numpy as np
from jax import lax
from jax.experimental import pallas as pl
from jax.experimental.pallas import tpu as pltpu
from jax.sharding import Mesh
from jax.sharding import PartitionSpec as P

SIDE = 8
CLUSTER_MOMENTUM = 64
W = 64
NU = 4
ITERS = 2
EXTENT = W + NU - 1
CELLS = CLUSTER_MOMENTUM * W
TAIL = CLUSTER_MOMENTUM * (NU - 1)
GROUP = SIDE * W
UP, DOWN, UP_TAIL, DOWN_TAIL, LOW = 0, CELLS, 2 * CELLS, 2 * CELLS + 256, 2 * CELLS + 512
PACKET = 2 * CELLS + 640
HALF = 128
ROWS = 2 * HALF


def gather_products(index_ref, ref, source_ref, up, down, stages):
    shift_major, shift_minor = index_ref[0] // SIDE, index_ref[0] % SIDE
    offset = index_ref[1]
    spins = ((UP, UP_TAIL, up), (DOWN, DOWN_TAIL, down))

    lanes = shift_minor * W + offset
    tiles, inner = lanes // 128, lanes % 128
    lane = lax.broadcasted_iota(jnp.int32, (HALF, 128), 1)
    near = lane + inner < 128
    kept = (lane & (W - 1)) + offset < W

    col = lax.broadcasted_iota(jnp.int32, (1, GROUP), 1)
    freq = (col & (W - 1)) + offset
    minor = (col // W + shift_minor) & (SIDE - 1)
    wanted = jnp.where(freq >= W, minor * (NU - 1) + freq - W, -256)
    row = lax.broadcasted_iota(jnp.int32, (256, GROUP), 0)

    def build(chosen, a, acc):
        moved = (a + shift_major) & (SIDE - 1)
        tail_select = jnp.where(row == wanted + moved * SIDE * (NU - 1), 1.0, 0.0)
        tail_select = tail_select.astype(jnp.bfloat16)
        for start, tail, held in chosen:
            wrapped = jnp.dot(
                ref[:, tail : tail + 256], tail_select, preferred_element_type=jnp.float32
            )
            turned = []
            for t in range(GROUP // 128):
                begin = start + moved * GROUP + ((t + tiles) & (GROUP // 128 - 1)) * 128
                far = ref[:, pl.ds(pl.multiple_of(begin, 128), 128)].astype(jnp.float32)
                turned.append(pltpu.roll(far, (128 - inner) & 127, 1))
            for t in range(GROUP // 128):
                here = pl.ds(pl.multiple_of(a * GROUP + t * 128, 128), 128)
                base = ref[:, pl.ds(pl.multiple_of(start + a * GROUP + t * 128, 128), 128)]
                other = jnp.where(near, turned[t], turned[(t + 1) % len(turned)])
                other = jnp.where(kept, other, wrapped[:, t * 128 : t * 128 + 128])
                made = (base.astype(jnp.float32) * other).astype(jnp.bfloat16)
                held[:, here] = made
                if held is up:
                    acc = acc + made.astype(jnp.float32) * source_ref[:, here]
        return acc

    acc = jnp.zeros((HALF, 128), jnp.float32)
    for chosen, copies in stages:
        for copy in copies:
            copy.wait()
        acc = lax.fori_loop(0, SIDE, functools.partial(build, spins[chosen]), acc)
    return acc


def prepare(index_ref, own_ref, source_ref, up_ref, down_ref, sums_ref):
    stages = ((slice(0, 2), ()),)
    sums_ref[...] = gather_products(index_ref, own_ref, source_ref, up_ref, down_ref, stages)


def three_rows(row):
    high = row.astype(jnp.bfloat16).astype(jnp.float32)
    middle = (row - high).astype(jnp.bfloat16).astype(jnp.float32)
    low = row - high - middle
    at = lax.broadcasted_iota(jnp.int32, (16, row.shape[1]), 0)
    return jnp.where(
        at == 0, high, jnp.where(at == 1, middle, jnp.where(at == 2, low, 0.0))
    )


def contract(
    index_ref, up_ref, down_ref, sums_ref, other_ref, source_ref, g4_ref, out_ref,
    up_other, down_other, left, stage, sems, raw, load_sems, norm, scale,
):
    site = index_ref[2]
    spans = (pl.ds(UP_TAIL, PACKET - UP_TAIL), pl.ds(UP, CELLS), pl.ds(DOWN, CELLS))
    loads = [
        pltpu.make_async_copy(other_ref.at[:, span], raw.at[:, span], load_sems.at[i])
        for i, span in enumerate(spans)
    ]
    for load in loads:
        load.start()
    stages = ((slice(0, 1), loads[:2]), (slice(1, 2), loads[2:]))
    sums = gather_products(index_ref, raw, source_ref, up_other, down_other, stages)
    first = jnp.concatenate(
        [jnp.sum(part.T, axis=0, keepdims=True) for part in (sums_ref[...], sums)], axis=1
    )
    ups, downs = (up_ref, up_other), (down_ref, down_other)

    pair = pl.ds(pl.multiple_of(site // 2 * 128, 128), 128)
    mine = []
    for ref in ups:
        left[...] = ref[:, pair].astype(jnp.float32).T
        mine.append(left[pl.ds(pl.multiple_of(site % 2 * W, W), W), :])
    lhs = jnp.concatenate([jnp.concatenate(mine, axis=1), three_rows(first)], axis=0)
    lhs = lhs.astype(jnp.bfloat16)

    copies = []
    last = [jnp.zeros((16, HALF), jnp.float32), jnp.zeros((16, HALF), jnp.float32)]
    for a in range(SIDE):
        here = pl.ds(a * GROUP, GROUP)
        right = jnp.concatenate([ref[:, here] for ref in downs], axis=0)
        both = jnp.dot(lhs, right, preferred_element_type=jnp.float32)
        stage[:, here] = both[:W] * norm
        copies.append(
            pltpu.make_async_copy(stage.at[:, here], g4_ref.at[:, here], sems.at[a])
        )
        copies[-1].start()
        moved = jnp.sum(both[W:], axis=0, keepdims=True)
        current = source_ref[:, here] + (scale * norm) * moved
        rows = three_rows(current).astype(jnp.bfloat16)
        for half, ref in enumerate(ups):
            last[half] += lax.dot_general(
                rows, ref[:, here], (((1,), (1,)), ((), ())),
                preferred_element_type=jnp.float32,
            )
    final = jnp.zeros((16, 128), jnp.float32)
    for part, ref in zip(last, downs):
        rows = three_rows(jnp.sum(part, axis=0, keepdims=True)).astype(jnp.bfloat16)
        final += jnp.dot(rows, ref[:, pair], preferred_element_type=jnp.float32)
    final = source_ref[:, pair] + (scale * norm) * jnp.sum(final, axis=0, keepdims=True)
    out_ref[...] = jnp.where(site % 2 == 1, final[:, W:], final[:, :W])
    for copy in copies:
        copy.wait()


def shards(green_up_blocks, green_down_blocks, nu_index, q_index, source):
    samples = ROWS
    norm = 1.0 / math.sqrt(samples)
    scale = 1.0 / (2.0 * math.sqrt(CELLS))

    both = jnp.concatenate(
        [green_up_blocks.reshape(1, -1), green_down_blocks.reshape(1, -1)], axis=0
    )
    sites = both.reshape(2 * CLUSTER_MOMENTUM, EXTENT)
    main = sites[:, :W].reshape(2 * CELLS)
    tails = sites[:, W:].reshape(2, TAIL)
    up_tail, down_tail = tails[0], tails[1]
    start = source.reshape(W)
    high = lax.reduce_precision(start, 8, 7)
    middle = lax.reduce_precision(start - high, 8, 7)
    low = start - high - middle
    packet = jnp.concatenate(
        [
            main,
            up_tail,
            high.astype(jnp.bfloat16),
            down_tail,
            middle.astype(jnp.bfloat16),
            low.astype(jnp.bfloat16),
            jnp.zeros((64,), jnp.bfloat16),
        ]
    ).reshape(PACKET // 128, 128)
    along = lax.all_to_all(jnp.broadcast_to(packet, (8,) + packet.shape), "z", 0, 0)
    rows = along.reshape(8, PACKET)
    own = lax.all_to_all(jnp.broadcast_to(rows, (16,) + rows.shape), ("x_hi", "x_lo", "y"), 0, 0)
    own = own.reshape(HALF, PACKET)
    other = lax.ppermute(own, "core", [(0, 1), (1, 0)])
    pieces = own.reshape(2, 2, 32, PACKET)[:, :, :, 2 * CELLS :]
    pieces = lax.dynamic_index_in_dim(pieces, lax.axis_index("x_lo"), 1, False)
    pieces = pieces.reshape(CLUSTER_MOMENTUM, 640).astype(jnp.float32)
    whole = (pieces[:, 192:256] + pieces[:, 448:512]) + pieces[:, 512:576]
    whole = whole.reshape(1, CELLS)
    site = (lax.axis_index("x_hi") * 4 + lax.axis_index("y")) * 8 + lax.axis_index("z")
    index = jnp.stack([q_index[0], nu_index[0], site.astype(jnp.int32)])
    vmem = pl.BlockSpec(memory_space=pltpu.VMEM)
    smem = pl.BlockSpec(memory_space=pltpu.SMEM)
    limit = pltpu.CompilerParams(vmem_limit_bytes=48 * 1024 * 1024)
    up, down, sums = pl.pallas_call(
        prepare,
        out_shape=(
            jax.ShapeDtypeStruct((HALF, CELLS), jnp.bfloat16),
            jax.ShapeDtypeStruct((HALF, CELLS), jnp.bfloat16),
            jax.ShapeDtypeStruct((HALF, 128), jnp.float32),
        ),
        in_specs=[smem, vmem, vmem],
        out_specs=(vmem, vmem, vmem),
        compiler_params=limit,
    )(index, own, whole)
    g4, answer = pl.pallas_call(
        functools.partial(contract, norm=norm, scale=scale),
        out_shape=(
            jax.ShapeDtypeStruct((W, CELLS), jnp.float32),
            jax.ShapeDtypeStruct((1, W), jnp.float32),
        ),
        in_specs=[smem, vmem, vmem, vmem, pl.BlockSpec(memory_space=pl.ANY), vmem],
        out_specs=(pl.BlockSpec(memory_space=pl.ANY), vmem),
        scratch_shapes=[
            pltpu.VMEM((HALF, CELLS), jnp.bfloat16),
            pltpu.VMEM((HALF, CELLS), jnp.bfloat16),
            pltpu.VMEM((128, HALF), jnp.float32),
            pltpu.VMEM((W, CELLS), jnp.float32),
            pltpu.SemaphoreType.DMA((SIDE,)),
            pltpu.VMEM((HALF, PACKET), jnp.bfloat16),
            pltpu.SemaphoreType.DMA((3,)),
        ],
        compiler_params=limit,
    )(index, up, down, sums, other, whole)
    return g4.reshape(1, W, CELLS), answer


def solution(mesh):
    fine = Mesh(
        np.asarray(mesh.devices).reshape(2, 4, 8, 2, 2), ("x_hi", "y", "z", "x_lo", "core")
    )
    walker, freq = ("x_hi", "y", "z"), ("x_lo", "core")
    in_specs = (
        P(walker, None, freq, None),
        P(walker, None, freq, None),
        P(freq),
        P(freq),
        P(freq, walker),
    )
    out_specs = (P(freq, walker, None), P(freq, walker))
    return jax.shard_map(shards, mesh=fine, in_specs=in_specs, out_specs=out_specs, check_vma=False)
```

```python
import functools
import math

import jax
import jax.numpy as jnp
import numpy as np
from jax import lax
from jax.experimental import pallas as pl
from jax.experimental.pallas import tpu as pltpu
from jax.sharding import Mesh
from jax.sharding import PartitionSpec as P

SIDE = 8
CLUSTER_MOMENTUM = 64
W = 64
NU = 4
ITERS = 2
EXTENT = W + NU - 1
CELLS = CLUSTER_MOMENTUM * W
TAIL = CLUSTER_MOMENTUM * (NU - 1)
GROUP = SIDE * W
UP, DOWN, UP_TAIL, DOWN_TAIL, LOW = 0, CELLS, 2 * CELLS, 2 * CELLS + 256, 2 * CELLS + 512
PACKET = 2 * CELLS + 640
HALF = 128
ROWS = 2 * HALF


def gather_products(index_ref, ref, source_ref, up, down, start_row, select, make):
    shift_major, shift_minor = index_ref[0] // SIDE, index_ref[0] % SIDE
    offset = index_ref[1]
    rows = pl.ds(start_row, HALF)

    lanes = shift_minor * W + offset
    tiles, inner = lanes // 128, lanes % 128
    lane = lax.broadcasted_iota(jnp.int32, (HALF, 128), 1)
    near = lane + inner < 128
    kept = (lane & (W - 1)) + offset < W

    col = lax.broadcasted_iota(jnp.int32, (1, GROUP), 1)
    freq = (col & (W - 1)) + offset
    minor = (col // W + shift_minor) & (SIDE - 1)
    wanted = jnp.where(freq >= W, minor * (NU - 1) + freq - W, -256)
    row = lax.broadcasted_iota(jnp.int32, (256, GROUP), 0)

    def build(a, acc):
        moved = (a + shift_major) & (SIDE - 1)
        block = pl.ds(pl.multiple_of(a * GROUP, GROUP), GROUP)
        if make:
            tail_select = jnp.where(row == wanted + moved * SIDE * (NU - 1), 1.0, 0.0)
            tail_select = tail_select.astype(jnp.bfloat16)
            select[:, block] = tail_select
        else:
            tail_select = select[:, block]
        for start, tail, held in ((UP, UP_TAIL, up), (DOWN, DOWN_TAIL, down)):
            wrapped = jnp.dot(
                ref[:, tail : tail + 256], tail_select, preferred_element_type=jnp.float32
            )
            turned = []
            for t in range(GROUP // 128):
                begin = start + moved * GROUP + ((t + tiles) & (GROUP // 128 - 1)) * 128
                far = ref[:, pl.ds(pl.multiple_of(begin, 128), 128)].astype(jnp.float32)
                turned.append(pltpu.roll(far, (128 - inner) & 127, 1))
            for t in range(GROUP // 128):
                here = pl.ds(pl.multiple_of(a * GROUP + t * 128, 128), 128)
                base = ref[:, pl.ds(pl.multiple_of(start + a * GROUP + t * 128, 128), 128)]
                other = jnp.where(near, turned[t], turned[(t + 1) % len(turned)])
                other = jnp.where(kept, other, wrapped[:, t * 128 : t * 128 + 128])
                made = (base.astype(jnp.float32) * other).astype(jnp.bfloat16)
                held[rows, here] = made
                if held is up:
                    acc = acc + made.astype(jnp.float32) * source_ref[:, here]
        return acc

    return lax.fori_loop(0, SIDE, build, jnp.zeros((HALF, 128), jnp.float32))


def prepare(index_ref, own_ref, source_ref, up_ref, down_ref, sums_ref, select_ref):
    sums_ref[...] = gather_products(
        index_ref, own_ref, source_ref, up_ref, down_ref, 0, select_ref, True
    )


def contract(
    index_ref, up_ref, down_ref, sums_ref, select_ref, other_ref, source_ref, g4_ref, out_ref,
    up_other, down_other, left, norm, scale,
):
    site = index_ref[2]
    sums = gather_products(
        index_ref, other_ref, source_ref, up_other, down_other, 0, select_ref, False
    )
    first = (
        jnp.sum(sums_ref[...], axis=1, keepdims=True),
        jnp.sum(sums, axis=1, keepdims=True),
    )
    ups, downs = (up_ref, up_other), (down_ref, down_other)

    pair = pl.ds(pl.multiple_of(site // 2 * 128, 128), 128)
    mine = []
    for half, ref in enumerate(ups):
        left[...] = ref[:, pair].astype(jnp.float32).T
        mine.append(left[pl.ds(pl.multiple_of(site % 2 * W, W), W), :].astype(jnp.bfloat16))

    def second(a, acc):
        here = pl.ds(pl.multiple_of(a * GROUP, GROUP), GROUP)
        right = [ref[:, here] for ref in downs]
        g4_ref[:, here] = (
            jnp.dot(mine[0], right[0], preferred_element_type=jnp.float32)
            + jnp.dot(mine[1], right[1], preferred_element_type=jnp.float32)
        ) * norm
        moved = sum(r.astype(jnp.float32) * f for r, f in zip(right, first))
        moved = jnp.sum(moved, axis=0, keepdims=True)
        current = source_ref[:, here] + (scale * norm) * moved
        made = []
        for ref, old in zip(ups, acc):
            weighted = ref[:, here].astype(jnp.float32) * current
            made.append(old + sum(weighted[:, i : i + 128] for i in range(0, GROUP, 128)))
        return tuple(made)

    zero = jnp.zeros((HALF, 128), jnp.float32)
    acc = lax.fori_loop(0, SIDE, second, (zero, zero))
    final = sum(
        ref[:, pair].astype(jnp.float32) * jnp.sum(part, axis=1, keepdims=True)
        for ref, part in zip(downs, acc)
    )
    final = source_ref[:, pair] + (scale * norm) * jnp.sum(final, axis=0, keepdims=True)
    out_ref[...] = jnp.where(site % 2 == 1, final[:, W:], final[:, :W])


def shards(green_up_blocks, green_down_blocks, nu_index, q_index, source):
    samples = ROWS
    norm = 1.0 / math.sqrt(samples)
    scale = 1.0 / (2.0 * math.sqrt(CELLS))

    both = jnp.concatenate(
        [green_up_blocks.reshape(1, -1), green_down_blocks.reshape(1, -1)], axis=0
    )
    sites = both.reshape(2 * CLUSTER_MOMENTUM, EXTENT)
    main = sites[:, :W].reshape(2 * CELLS)
    tails = sites[:, W:].reshape(2, TAIL)
    up_tail, down_tail = tails[0], tails[1]
    start = source.reshape(W)
    high = lax.reduce_precision(start, 8, 7)
    middle = lax.reduce_precision(start - high, 8, 7)
    low = start - high - middle
    packet = jnp.concatenate(
        [
            main,
            up_tail,
            high.astype(jnp.bfloat16),
            down_tail,
            middle.astype(jnp.bfloat16),
            low.astype(jnp.bfloat16),
            jnp.zeros((64,), jnp.bfloat16),
        ]
    ).reshape(PACKET // 128, 128)
    along = lax.all_to_all(jnp.broadcast_to(packet, (8,) + packet.shape), "z", 0, 0)
    rows = along.reshape(8, PACKET)
    own = lax.all_to_all(jnp.broadcast_to(rows, (16,) + rows.shape), ("x_hi", "x_lo", "y"), 0, 0)
    own = own.reshape(HALF, PACKET)
    other = lax.ppermute(own, "core", [(0, 1), (1, 0)])
    pieces = own.reshape(2, 2, 32, PACKET)[:, :, :, 2 * CELLS :]
    pieces = lax.dynamic_index_in_dim(pieces, lax.axis_index("x_lo"), 1, False)
    pieces = pieces.reshape(CLUSTER_MOMENTUM, 640).astype(jnp.float32)
    whole = (pieces[:, 192:256] + pieces[:, 448:512]) + pieces[:, 512:576]
    whole = whole.reshape(1, CELLS)
    site = (lax.axis_index("x_hi") * 4 + lax.axis_index("y")) * 8 + lax.axis_index("z")
    index = jnp.stack([q_index[0], nu_index[0], site.astype(jnp.int32)])
    vmem = pl.BlockSpec(memory_space=pltpu.VMEM)
    smem = pl.BlockSpec(memory_space=pltpu.SMEM)
    limit = pltpu.CompilerParams(vmem_limit_bytes=48 * 1024 * 1024)
    up, down, sums, select = pl.pallas_call(
        prepare,
        out_shape=(
            jax.ShapeDtypeStruct((HALF, CELLS), jnp.bfloat16),
            jax.ShapeDtypeStruct((HALF, CELLS), jnp.bfloat16),
            jax.ShapeDtypeStruct((HALF, 128), jnp.float32),
            jax.ShapeDtypeStruct((256, CELLS), jnp.bfloat16),
        ),
        in_specs=[smem, vmem, vmem],
        out_specs=(vmem, vmem, vmem, vmem),
        compiler_params=limit,
    )(index, own, whole)
    g4, answer = pl.pallas_call(
        functools.partial(contract, norm=norm, scale=scale),
        out_shape=(
            jax.ShapeDtypeStruct((W, CELLS), jnp.float32),
            jax.ShapeDtypeStruct((1, W), jnp.float32),
        ),
        in_specs=[smem, vmem, vmem, vmem, vmem, vmem, vmem],
        out_specs=(vmem, vmem),
        scratch_shapes=[
            pltpu.VMEM((HALF, CELLS), jnp.bfloat16),
            pltpu.VMEM((HALF, CELLS), jnp.bfloat16),
            pltpu.VMEM((128, HALF), jnp.float32),
        ],
        compiler_params=limit,
    )(index, up, down, sums, select, other, whole)
    return g4.reshape(1, W, CELLS), answer


def solution(mesh):
    fine = Mesh(
        np.asarray(mesh.devices).reshape(2, 4, 8, 2, 2), ("x_hi", "y", "z", "x_lo", "core")
    )
    walker, freq = ("x_hi", "y", "z"), ("x_lo", "core")
    in_specs = (
        P(walker, None, freq, None),
        P(walker, None, freq, None),
        P(freq),
        P(freq),
        P(freq, walker),
    )
    out_specs = (P(freq, walker, None), P(freq, walker))
    return jax.shard_map(shards, mesh=fine, in_specs=in_specs, out_specs=out_specs, check_vma=False)
```
